128 devices in a mesh: comm: 4 (over x), wide: 32 (over y, z, core).
Axes of the slice: x: 4, y: 4, z: 4, core: 2. Of those that a mesh axis runs over, the one named last changes fastest.
Arguments:
- feats: bfloat16 [256, 768, 768], P(('comm', 'wide')), may hold values from -6 to 6
- tiles: bfloat16 [256, 3, 768, 768], P(('comm', 'wide')), may hold values from -0.15625 to 0.15625
- tile_src: int32 [256, 3], P(('comm', 'wide')), may hold values from 0 to 5
- tile_count: int32 [256], P(('comm', 'wide')), may hold values from 1 to 3
- request: int32 [128, 4], P(('comm', 'wide')), may hold values from 0 to 1
- z_old: bfloat16 [256, 768, 1024], P(('comm', 'wide')), may hold values from -6 to 6
- dual: bfloat16 [256, 768, 1024], P(('comm', 'wide')), may hold values from -6 to 6
- target: bfloat16 [256, 768, 1024], P(('comm', 'wide')), may hold values from 0 to 2
- w_rows: bfloat16 [768, 1024], P('wide'), may hold values from -0.21875 to 0.21875
- rho: float32 [1024], replicated, may hold values from 0.3 to 4
- beta: float32 [1024], replicated, may hold values from 0.3 to 4
Outputs:
- new_z: bfloat16 [256, 768, 1024], P(('comm', 'wide'))
- new_dual: bfloat16 [256, 768, 1024], P(('comm', 'wide'))
- weight_grad: float32 [768, 1024], P('wide')
The draws below stay inside these ranges and needn't reach their ends.
Inputs may be any that keep to these rules, and one draw needn't show every extreme that they name: `tile_src`: entries beyond tile_count of a community are not read.
All inputs are finite; a program needn't handle non-finite values.
Results may differ from the reference program's by a relative error of at most 0.0095.
Values may be sent and summed in bfloat16 or wider, within the bound.
No kernel may reach another device: no remote copies, remote signals or barrier semaphores. Data moves between devices by JAX's collectives and lax.ppermute only.
A program may use at most 128 MiB of HBM per device.

```python
import math
import jax
import jax.numpy as jnp
from jax import lax

C = 768
F = 768
H = 1024
TILES = 3
COMM_DEV = 2
COMMS = 256
NODES = 196608
N_COMM = 4
N_WIDE = 32
DEVICES = 128


def plant(result, rng, low, high):
    shape = result.shape
    place = [jax.random.randint(jax.random.fold_in(rng, axis), (), 0, shape[axis]) for axis in range(len(shape))]
    result = result.at[tuple(place)].set(low)
    longest = shape.index(max(shape))
    place[longest] = (place[longest] + 1) % shape[longest]
    return result.at[tuple(place)].set(high)


def shard_levels(own_key, shape, pieces, low, largest):
    def one(dim, shards_of):
        draws = jax.random.uniform(jax.random.fold_in(jax.random.fold_in(own_key, 6), dim), (shards_of,), jnp.float32, low / len(pieces), largest / len(pieces))
        return jnp.repeat(jnp.exp(draws), shape[dim] // shards_of).reshape((-1,) + (1,) * (len(shape) - dim - 1))

    factor_of = one(*pieces[0])
    for cut in pieces[1:]:
        factor_of = factor_of * one(*cut)
    return factor_of


def gaussian(key, shape, spread, most, shards=(), kind=jnp.bfloat16):
    values = jax.random.normal(key, shape, jnp.float32) * spread
    if len(shards) > 0:
        values = shard_levels(key, shape, shards, -0.22, 0.18) * values
    return jnp.clip(values, min=-most, max=most).astype(kind)


def setup_inputs(seed: int = 0) -> dict:
    keys = jax.random.split(jax.random.key(seed), 12)
    return {
        "feats": gaussian(keys[0], (COMMS, C, F), 1.0, 6.0, ((0, 128),)),
        "tiles": gaussian(keys[1], (COMMS, TILES, C, C), (C * 2) ** -0.5, 0.15625, ((0, 128),)),
        "tile_src": plant(jax.random.randint(keys[2], (COMMS, TILES), 0, COMM_DEV + N_COMM), jax.random.fold_in(keys[2], 1), 0, (COMM_DEV + N_COMM) - 1).astype(jnp.int32),
        "tile_count": plant(jax.random.randint(keys[3], (COMMS,), 1, TILES + 1), jax.random.fold_in(keys[3], 1), 1, TILES).astype(jnp.int32),
        "request": plant(jax.random.randint(keys[4], (DEVICES, N_COMM), 0, COMM_DEV), jax.random.fold_in(keys[4], 1), 0, COMM_DEV - 1).astype(jnp.int32),
        "z_old": gaussian(keys[5], (COMMS, C, H), 1.0, 6.0, ((0, 128),)),
        "dual": gaussian(keys[6], (COMMS, C, H), 1.0, 6.0, ((0, 128),)),
        "target": jnp.clip(2.0 * jax.random.uniform(keys[7], (COMMS, C, H), jnp.float32) ** shard_levels(keys[7], (COMMS, C, H), ((0, 128),), -0.2, 0.2), 0.0, 2.0).astype(jnp.bfloat16),
        "w_rows": gaussian(keys[8], (F, H), F ** -0.5, 0.21875, ((0, 32),)),
        "rho": jnp.clip(jnp.exp(jax.random.uniform(keys[9], (H,), jnp.float32, math.log(0.3), math.log(4.0))), 0.3, 4.0),
        "beta": jnp.clip(jnp.exp(jax.random.uniform(keys[10], (H,), jnp.float32, math.log(0.3), math.log(4.0))), 0.3, 4.0),
    }


def reference(feats, tiles, tile_src, tile_count, request, z_old, dual, target, w_rows, rho, beta):
    owner = jnp.arange(COMMS, dtype=jnp.int32) // COMM_DEV
    wide_pos = owner % N_WIDE
    slot = jnp.maximum(tile_src - COMM_DEV, 0).astype(jnp.int32)
    peer_dev = slot * N_WIDE + wide_pos[:, None]
    picked = request[owner[:, None], slot]
    remote = peer_dev * COMM_DEV + picked
    local = owner[:, None] * COMM_DEV + tile_src
    source = jnp.where(tile_src < COMM_DEV, local, remote).astype(jnp.int32)
    live = (jnp.arange(TILES, dtype=jnp.int32)[None, :] < tile_count[:, None]).astype(jnp.float32)

    def one(args):
        tile_set, index, keep = args
        blocks = feats[index].astype(jnp.float32) * keep[:, None, None]
        total = jnp.einsum('tij,tjf->if', tile_set.astype(jnp.float32), blocks)
        return total.astype(jnp.bfloat16)
    agg = lax.map(one, (tiles, source, live))
    flat = agg.reshape(-1, F)
    pre = jnp.dot(flat, w_rows, preferred_element_type=jnp.float32).reshape(COMMS, C, H)
    shifted = pre + dual.astype(jnp.float32) / rho
    active = (rho * shifted + beta * target.astype(jnp.float32)) / (rho + beta)
    znew = jnp.where(z_old > 0, active, shifted)
    new_dual = (dual.astype(jnp.float32) + rho * (pre - znew)).astype(jnp.bfloat16)
    grad = jnp.einsum('nf,nh->fh', flat.astype(jnp.float32), new_dual.reshape(-1, H).astype(jnp.float32))
    grad = grad * (1.0 / math.sqrt(NODES))
    return (znew.astype(jnp.bfloat16), new_dual, grad)
```

```python
import functools
import math

import jax
import jax.numpy as jnp
from jax import lax
from jax.experimental import pallas as pl
from jax.experimental.pallas import tpu as pltpu
from jax.sharding import PartitionSpec as P

ROWS = 256
COLS = 256
LIMIT = 24 * 2**20
SMEM = pl.BlockSpec(memory_space=pltpu.SMEM)
VMEM = pl.BlockSpec(memory_space=pltpu.VMEM)
ANY = pl.BlockSpec(memory_space=pl.ANY)


def shifted(x, axis, to):
    size = lax.axis_size(axis)
    return lax.ppermute(x, axis, [(i, to(i)) for i in range(size)])


def place(w):
    return w // 8, w // 2 % 4, w % 2


def along_comm(x, step):
    return shifted(x, "comm", lambda i: (i + step) % 4)


def along_core(x):
    return shifted(x, "wide", lambda w: w ^ 1)


def along_z(x, step):
    return shifted(x, "wide", lambda w: w // 8 * 8 + (w // 2 % 4 + step) % 4 * 2 + w % 2)


def along_y(x, step):
    return shifted(x, "wide", lambda w: (w // 8 + step) % 4 * 8 + w % 8)


def own_products(src, count, request, feats, tiles, acc, buf, sems):
    me = lax.axis_index("comm")
    comms, slots = tiles.shape[0], tiles.shape[1]
    local = feats.shape[0]

    def wanted(k, t):
        source = src[k, t]
        own = (source < local) | (source == local + me)
        return (t < count[k]) & own

    def copy(k, t):
        return pltpu.make_async_copy(tiles.at[k, t], buf.at[k, t], sems.at[k, t])

    for k in range(comms):
        for t in range(slots):
            pl.when(wanted(k, t))(copy(k, t).start)
    for k in range(comms):
        acc[k] = jnp.zeros(acc.shape[1:], jnp.float32)
        for t in range(slots):

            @pl.when(wanted(k, t))
            def _():
                copy(k, t).wait()
                source = src[k, t]
                block = jnp.where(source < local, source, request[0, me])

                @pl.loop(0, acc.shape[1] // ROWS)
                def _(i):
                    rows = pl.ds(pl.multiple_of(i * ROWS, ROWS), ROWS)
                    acc[k, rows, :] += jnp.dot(
                        buf[k, t, rows, :], feats[block], preferred_element_type=jnp.float32
                    )


def call_own_products(src, count, request, feats, tiles):
    comms, slots, nodes, _ = tiles.shape
    width = feats.shape[2]
    return pl.pallas_call(
        own_products,
        out_shape=jax.ShapeDtypeStruct((comms, nodes, width), jnp.float32),
        in_specs=[SMEM, SMEM, SMEM, VMEM, ANY],
        out_specs=VMEM,
        scratch_shapes=[
            pltpu.VMEM(tiles.shape, tiles.dtype),
            pltpu.SemaphoreType.DMA((comms, slots)),
        ],
        compiler_params=pltpu.CompilerParams(vmem_limit_bytes=LIMIT),
        cost_estimate=pl.CostEstimate(
            flops=3 * 2 * nodes * nodes * width, bytes_accessed=4 * 2**20, transcendentals=0
        ),
        name="own_products",
    )(src, count, request, feats, tiles)


def update(
    src, count, tiles, from1, from2, from3, acc, weight, z_old, dual, target, rho, beta,
    new_z, new_dual, agg, buf, total, zbuf, dbuf, sems, osems,
):
    me = lax.axis_index("comm")
    comms, slots, nodes, _ = tiles.shape
    local = comms
    hidden = weight.shape[1]
    per = nodes // ROWS
    steps = comms * per

    def step_of(k, t):
        source = src[k, t]
        rel = lax.rem(source - local - me + 8, 4)
        live = (t < count[k]) & (source >= local) & (rel > 0)
        return live, rel

    def copy(k, t):
        return pltpu.make_async_copy(tiles.at[k, t], buf.at[k, t], sems.at[k, t])

    def out_copies(i, slot):
        rows = pl.ds(pl.multiple_of(i * ROWS, ROWS), ROWS)
        return (
            pltpu.make_async_copy(zbuf.at[slot], new_z.at[rows, :], osems.at[0, slot]),
            pltpu.make_async_copy(dbuf.at[slot], new_dual.at[rows, :], osems.at[1, slot]),
        )

    for k in range(comms):
        for t in range(slots):
            pl.when(step_of(k, t)[0])(copy(k, t).start)

    @pl.loop(0, steps)
    def _(i):
        k = i // per
        first = i - k * per == 0
        rows = pl.ds(pl.multiple_of((i - k * per) * ROWS, ROWS), ROWS)
        flat = pl.ds(pl.multiple_of(i * ROWS, ROWS), ROWS)
        slot = lax.rem(i, 2)
        total[...] = acc[k, rows, :]
        for t in range(slots):
            live, rel = step_of(k, t)

            @pl.when(live & first)
            def _():
                copy(k, t).wait()

            for r, block in ((1, from1), (2, from2), (3, from3)):

                @pl.when(live & (rel == r))
                def _():
                    total[...] += jnp.dot(
                        buf[k, t, rows, :], block[...], preferred_element_type=jnp.float32
                    )

        part = total[...].astype(jnp.bfloat16)
        agg[flat, :] = part

        @pl.when(i >= 2)
        def _():
            for c in out_copies(i - 2, slot):
                c.wait()

        for h in range(hidden // COLS):
            cols = slice(h * COLS, (h + 1) * COLS)
            r, b = rho[:, cols], beta[:, cols]
            share = b / (r + b)
            pre = jnp.dot(part, weight[:, cols], preferred_element_type=jnp.float32)
            v = pre + dual[flat, cols].astype(jnp.float32) * (1.0 / r)
            gap = jnp.where(
                z_old[flat, cols].astype(jnp.float32) > 0,
                (v - target[flat, cols].astype(jnp.float32)) * share,
                0.0,
            )
            zbuf[slot, :, cols] = (v - gap).astype(jnp.bfloat16)
            dbuf[slot, :, cols] = (r * gap).astype(jnp.bfloat16)
        for c in out_copies(i, slot):
            c.start()

    for i in (steps - 2, steps - 1):
        for c in out_copies(i, i % 2):
            c.wait()


def call_update(src, count, tiles, blocks, acc, weight, z_old, dual, target, rho, beta):
    comms, slots, nodes, _ = tiles.shape
    width, hidden = weight.shape
    flat = comms * nodes
    return pl.pallas_call(
        update,
        out_shape=(
            jax.ShapeDtypeStruct((flat, hidden), jnp.bfloat16),
            jax.ShapeDtypeStruct((flat, hidden), jnp.bfloat16),
            jax.ShapeDtypeStruct((flat, width), jnp.bfloat16),
        ),
        in_specs=[SMEM, SMEM, ANY] + [VMEM] * 10,
        out_specs=(ANY, ANY, VMEM),
        scratch_shapes=[
            pltpu.VMEM(tiles.shape, tiles.dtype),
            pltpu.VMEM((ROWS, width), jnp.float32),
            pltpu.VMEM((2, ROWS, hidden), jnp.bfloat16),
            pltpu.VMEM((2, ROWS, hidden), jnp.bfloat16),
            pltpu.SemaphoreType.DMA((comms, slots)),
            pltpu.SemaphoreType.DMA((2, 2)),
        ],
        compiler_params=pltpu.CompilerParams(vmem_limit_bytes=LIMIT),
        cost_estimate=pl.CostEstimate(
            flops=2 * flat * width * hidden + 3 * 2 * nodes * nodes * width,
            bytes_accessed=12 * 2**20,
            transcendentals=0,
        ),
        name="update",
    )(src, count, tiles, *blocks, acc, weight, z_old, dual, target, rho[None], beta[None])


def reduced(grad, factor):
    width, hidden = grad.shape
    y, z, core = place(lax.axis_index("wide"))
    pick = functools.partial(lax.dynamic_index_in_dim, keepdims=False)
    f32 = lambda x: x.astype(jnp.float32)
    parts = grad.reshape(4, 4, 2, width // 32, hidden)
    held = f32(pick(parts, core, 2)) + f32(along_core(pick(parts, 1 - core, 2)))
    parts = held.astype(jnp.bfloat16)
    held = f32(pick(parts, z, 1))
    for step in (1, 2, 3):
        held = held + f32(along_z(pick(parts, (z + step) % 4, 1), step))
    parts = held.astype(jnp.bfloat16)
    held = f32(pick(parts, y, 0))
    for step in (1, 2, 3):
        held = held + f32(along_y(pick(parts, (y + step) % 4, 0), step))
    mine = held.astype(jnp.bfloat16)
    held = f32(mine)
    for step in (1, 2, 3):
        held = held + f32(along_comm(mine, step))
    return held * factor


def local(feats, tiles, tile_src, tile_count, request, z_old, dual, target, w_rows, rho, beta):
    comms, nodes, width = feats.shape
    hidden = w_rows.shape[1]
    me = lax.axis_index("comm")
    blocks = []
    for rel in (1, 2, 3):
        step = 4 - rel
        asked = along_comm(request, rel)[0, me]
        block = lax.dynamic_index_in_dim(feats, asked, 0, keepdims=False)
        blocks.append(along_comm(block, step))
    acc = call_own_products(tile_src, tile_count, request, feats, tiles)
    weight = lax.all_gather(w_rows, "wide", axis=0, tiled=True)
    flat = lambda x: x.reshape(comms * nodes, hidden)
    new_z, new_dual, agg = call_update(
        tile_src, tile_count, tiles, blocks, acc, weight,
        flat(z_old), flat(dual), flat(target), rho, beta,
    )
    grad = jnp.einsum("nf,nh->fh", agg, new_dual, preferred_element_type=jnp.float32)
    total_nodes = comms * nodes * lax.axis_size("comm") * lax.axis_size("wide")
    grad = reduced(grad.astype(jnp.bfloat16), 1.0 / math.sqrt(total_nodes))
    return new_z.reshape(z_old.shape), new_dual.reshape(z_old.shape), grad


def solution(mesh):
    split = P(("comm", "wide"))
    in_specs = (split,) * 8 + (P("wide"), P(), P())
    out_specs = (split, split, P("wide"))
    return jax.shard_map(local, mesh=mesh, in_specs=in_specs, out_specs=out_specs, check_vma=False)
```

```python
import functools
import math

import jax
import jax.numpy as jnp
from jax import lax
from jax.experimental import pallas as pl
from jax.experimental.pallas import tpu as pltpu
from jax.sharding import PartitionSpec as P

ROWS = 256
COLS = 256
FEATS = 384
CUTS = (512, 256, 512)
SMALL = pl.CostEstimate(flops=2**20, bytes_accessed=2**16, transcendentals=0)
SMEM = pl.BlockSpec(memory_space=pltpu.SMEM)
VMEM = pl.BlockSpec(memory_space=pltpu.VMEM)
HBM = pl.BlockSpec(memory_space=pltpu.HBM)


def shifted(x, axis, to):
    size = lax.axis_size(axis)
    return lax.ppermute(x, axis, [(i, to(i)) for i in range(size)])


def place(w):
    return w // 8, w // 2 % 4, w % 2


def along_comm(x, step):
    return shifted(x, "comm", lambda i: (i + step) % 4)


def along_core(x):
    return shifted(x, "wide", lambda w: w ^ 1)


def along_z(x, step):
    return shifted(x, "wide", lambda w: w // 8 * 8 + (w // 2 % 4 + step) % 4 * 2 + w % 2)


def along_y(x, step):
    return shifted(x, "wide", lambda w: (w // 8 + step) % 4 * 8 + w % 8)


def in_hbm(x):
    return pltpu.with_memory_space_constraint(x, pltpu.HBM)


def me_on_comm():
    return lax.axis_index("comm")


def choose(ask1, ask2, ask3, feats, *refs):
    outs, sems = refs[:-1], refs[-1]
    me = me_on_comm()
    copies = []
    for n, ask in enumerate((ask1, ask2, ask3)):
        asked, cut = ask[0, me], CUTS[n]
        for part, cols in enumerate((slice(0, cut), slice(cut, feats.shape[2]))):
            copies.append(
                pltpu.make_async_copy(
                    feats.at[asked, :, cols], outs[2 * n + part], sems.at[2 * n + part]
                )
            )
    for c in copies:
        c.start()
    for c in copies:
        c.wait()


def call_choose(asks, feats):
    nodes, width = feats.shape[1:]
    shapes = [
        jax.ShapeDtypeStruct((nodes, cols), feats.dtype)
        for cut in CUTS
        for cols in (cut, width - cut)
    ]
    return pl.pallas_call(
        choose,
        out_shape=shapes,
        in_specs=[SMEM] * 3 + [HBM],
        out_specs=[VMEM] * len(shapes),
        scratch_shapes=[pltpu.SemaphoreType.DMA((len(shapes),))],
        compiler_params=pltpu.CompilerParams(vmem_limit_bytes=2**20),
        cost_estimate=SMALL,
        name="choose",
    )(*asks, in_hbm(feats))


def own_products(
    src, count, request, feats, tiles, z_old, dual, target,
    acc, far, zs, ds, ts, buf, sems, fsems, xsems,
):
    me = me_on_comm()
    comms, slots = tiles.shape[0], tiles.shape[1]
    local = feats.shape[0]

    def live(k, t):
        return t < count[k]

    def own(k, t):
        source = src[k, t]
        return (source < local) | (source == local + me)

    def near_copy(k, t):
        return pltpu.make_async_copy(tiles.at[k, t], buf.at[k, t], sems.at[k, t])

    def far_copy(k, t):
        return pltpu.make_async_copy(tiles.at[k, t], far.at[k, t], fsems.at[k, t])

    staged = [
        pltpu.make_async_copy(a, b, xsems.at[n])
        for n, (a, b) in enumerate(((z_old, zs), (dual, ds), (target, ts)))
    ]
    for k in range(comms):
        for t in range(slots):
            pl.when(live(k, t) & own(k, t))(near_copy(k, t).start)
    for k in range(comms):
        for t in range(slots):
            pl.when(live(k, t) & ~own(k, t))(far_copy(k, t).start)
    for c in staged:
        c.start()
    for k in range(comms):
        acc[k] = jnp.zeros(acc.shape[1:], jnp.float32)
        for t in range(slots):

            @pl.when(live(k, t) & own(k, t))
            def _():
                near_copy(k, t).wait()
                source = src[k, t]
                block = jnp.where(source < local, source, request[0, me])

                @pl.loop(0, acc.shape[1] // ROWS)
                def _(i):
                    rows = pl.ds(pl.multiple_of(i * ROWS, ROWS), ROWS)
                    acc[k, rows, :] += jnp.dot(
                        buf[k, t, rows, :], feats[block], preferred_element_type=jnp.float32
                    )

    for k in range(comms):
        for t in range(slots):
            pl.when(live(k, t) & ~own(k, t))(far_copy(k, t).wait)
    for c in staged:
        c.wait()


def call_own_products(src, count, request, feats, tiles, z_old, dual, target):
    comms, slots, nodes, _ = tiles.shape
    width = feats.shape[2]
    like = lambda a: jax.ShapeDtypeStruct(a.shape, a.dtype)
    return pl.pallas_call(
        own_products,
        out_shape=(
            jax.ShapeDtypeStruct((comms, nodes, width), jnp.float32),
            like(tiles), like(z_old), like(dual), like(target),
        ),
        in_specs=[SMEM, SMEM, SMEM, VMEM] + [HBM] * 4,
        out_specs=(VMEM,) * 5,
        scratch_shapes=[
            pltpu.VMEM(tiles.shape, tiles.dtype),
            pltpu.SemaphoreType.DMA((comms, slots)),
            pltpu.SemaphoreType.DMA((comms, slots)),
            pltpu.SemaphoreType.DMA((3,)),
        ],
        compiler_params=pltpu.CompilerParams(vmem_limit_bytes=10 * 2**20),
        cost_estimate=SMALL,
        name="own_products",
    )(src, count, request, feats, *map(in_hbm, (tiles, z_old, dual, target)))


def relation(src, count, k, t, local):
    rel = lax.rem(src[k, t] - local - me_on_comm() + 8, 4)
    return (t < count[k]) & (src[k, t] >= local) & (rel > 0), rel


def head_products(src, count, far, head1, head2, head3, before, acc):
    comms, slots, nodes, _ = far.shape
    for k in range(comms):
        for t in range(slots):
            live, rel = relation(src, count, k, t, comms)
            for r, (block, cut) in enumerate(zip((head1, head2, head3), CUTS), 1):

                @pl.when(live & (rel == r))
                def _():
                    @pl.loop(0, nodes // ROWS)
                    def _(i):
                        rows = pl.ds(pl.multiple_of(i * ROWS, ROWS), ROWS)
                        acc[k, rows, :cut] += jnp.dot(
                            far[k, t, rows, :], block[...], preferred_element_type=jnp.float32
                        )


def call_head_products(src, count, far, heads, acc):
    return pl.pallas_call(
        head_products,
        out_shape=jax.ShapeDtypeStruct(acc.shape, acc.dtype),
        in_specs=[SMEM, SMEM] + [VMEM] * 5,
        out_specs=VMEM,
        input_output_aliases={6: 0},
        compiler_params=pltpu.CompilerParams(vmem_limit_bytes=4 * 2**20),
        cost_estimate=SMALL,
        name="head_products",
    )(src, count, far, *heads, acc)


def update(
    src, count, far, from1, from2, from3, acc, weight, z_old, dual, target, rho, beta,
    new_z, new_dual, keep, send, agg, total, zbuf, dbuf, osems,
):
    core = my_core()
    comms, slots, nodes, _ = far.shape
    width, hidden = weight.shape
    per = nodes // ROWS
    steps = comms * per

    def out_copies(i):
        rows = pl.ds(pl.multiple_of(i * ROWS, ROWS), ROWS)
        return (
            pltpu.make_async_copy(zbuf.at[rows, :], new_z.at[rows, :], osems.at[0, i]),
            pltpu.make_async_copy(dbuf.at[rows, :], new_dual.at[rows, :], osems.at[1, i]),
        )

    @pl.loop(0, steps)
    def _(i):
        k = i // per
        rows = pl.ds(pl.multiple_of((i - k * per) * ROWS, ROWS), ROWS)
        flat = pl.ds(pl.multiple_of(i * ROWS, ROWS), ROWS)
        total[...] = acc[k, rows, :]
        for t in range(slots):
            live, rel = relation(src, count, k, t, comms)
            for r, (block, cut) in enumerate(zip((from1, from2, from3), CUTS), 1):

                @pl.when(live & (rel == r))
                def _():
                    total[:, cut:] += jnp.dot(
                        far[k, t, rows, :], block[...], preferred_element_type=jnp.float32
                    )

        part = total[...].astype(jnp.bfloat16)
        agg[flat, :] = part
        for h in range(hidden // COLS):
            cols = slice(h * COLS, (h + 1) * COLS)
            r, b = rho[:, cols], beta[:, cols]
            share = b / (r + b)
            pre = jnp.dot(part, weight[:, cols], preferred_element_type=jnp.float32)
            v = pre + dual[flat, cols].astype(jnp.float32) * (1.0 / r)
            gap = jnp.where(
                z_old[flat, cols].astype(jnp.float32) > 0,
                (v - target[flat, cols].astype(jnp.float32)) * share,
                0.0,
            )
            zbuf[flat, cols] = (v - gap).astype(jnp.bfloat16)
            dbuf[flat, cols] = (r * gap).astype(jnp.bfloat16)
        for c in out_copies(i):
            c.start()

    piece = keep.shape[1]
    group = FEATS // piece

    for f in range(width // FEATS):
        grad = lax.dot_general(
            agg[:, f * FEATS:(f + 1) * FEATS], dbuf[...],
            (((0,), (0,)), ((), ())), preferred_element_type=jnp.float32,
        ).astype(jnp.bfloat16)
        for n in range(group):
            at = f * group + n
            rows = grad[n * piece:(n + 1) * piece]

            @pl.when(core == at % 2)
            def _():
                keep[at // 2] = rows

            @pl.when(core != at % 2)
            def _():
                send[at // 2] = rows

    @pl.loop(0, steps)
    def _(i):
        for c in out_copies(i):
            c.wait()


def call_update(src, count, far, blocks, acc, weight, z_old, dual, target, rho, beta, piece):
    comms, slots, nodes, _ = far.shape
    width, hidden = weight.shape
    flat = comms * nodes
    steps = flat // ROWS
    wide = jax.ShapeDtypeStruct((flat, hidden), jnp.bfloat16)
    half = jax.ShapeDtypeStruct((width // piece // 2, piece, hidden), jnp.bfloat16)
    return pl.pallas_call(
        update,
        out_shape=(wide, wide, half, half),
        in_specs=[SMEM, SMEM] + [VMEM] * 11,
        out_specs=(HBM, HBM, VMEM, VMEM),
        scratch_shapes=[
            pltpu.VMEM((flat, width), jnp.bfloat16),
            pltpu.VMEM((ROWS, width), jnp.float32),
            pltpu.VMEM((flat, hidden), jnp.bfloat16),
            pltpu.VMEM((flat, hidden), jnp.bfloat16),
            pltpu.SemaphoreType.DMA((2, steps)),
        ],
        compiler_params=pltpu.CompilerParams(vmem_limit_bytes=18 * 2**20),
        cost_estimate=pl.CostEstimate(
            flops=4 * flat * width * hidden + 3 * 2 * nodes * nodes * width,
            bytes_accessed=6 * 2**20,
            transcendentals=0,
        ),
        name="update",
    )(src, count, far, *blocks, acc, weight, z_old, dual, target, rho[None], beta[None])


def arrange(first, *refs):
    out = refs[-1]
    for d, part in enumerate(refs[:-1]):
        out[lax.rem(first() + d, len(refs) - 1)] = part[...]


def call_arrange(first, parts, name):
    shape = jax.ShapeDtypeStruct((len(parts), *parts[0].shape), parts[0].dtype)
    return pl.pallas_call(
        functools.partial(arrange, first),
        out_shape=shape,
        in_specs=[VMEM] * len(parts),
        out_specs=VMEM,
        compiler_params=pltpu.CompilerParams(vmem_limit_bytes=2**20),
        cost_estimate=SMALL,
        name=name,
    )(*parts)


def my_y():
    return lax.axis_index("wide") // 8


def my_z():
    return lax.rem(lax.axis_index("wide") // 2, 4)


def my_core():
    return lax.rem(lax.axis_index("wide"), 2)


def pair(mine, other, out):
    core = my_core()

    @pl.loop(0, mine.shape[0])
    def _(i):
        out[i, core] = mine[i]
        out[i, 1 - core] = other[i]


def call_pair(mine, other):
    groups, piece, hidden = mine.shape
    return pl.pallas_call(
        pair,
        out_shape=jax.ShapeDtypeStruct((groups, 2, piece, hidden), mine.dtype),
        in_specs=[VMEM, VMEM],
        out_specs=VMEM,
        compiler_params=pltpu.CompilerParams(vmem_limit_bytes=2**20),
        cost_estimate=SMALL,
        name="pair_rows",
    )(mine, other)


def weight_of_z(rows):
    return call_arrange(my_z, [rows] + [along_z(rows, 4 - d) for d in (1, 2, 3)], "rows_of_z")


def whole_weight(parts):
    piece, hidden = parts.shape[1:]
    parts = call_arrange(my_y, [parts] + [along_y(parts, 4 - d) for d in (1, 2, 3)], "rows_of_y")
    parts = parts.reshape(16, piece, hidden)
    return call_pair(parts, along_core(parts)).reshape(32 * piece, hidden)


def reduced(keep, send, factor):
    y, z, _ = place(lax.axis_index("wide"))
    pick = functools.partial(lax.dynamic_index_in_dim, keepdims=False)
    f32 = lambda x: x.astype(jnp.float32)
    parts = (f32(keep) + f32(along_core(send))).astype(jnp.bfloat16)
    parts = parts.reshape(4, 4, *keep.shape[1:])
    held = f32(pick(parts, z, 1))
    for step in (1, 2, 3):
        held = held + f32(along_z(pick(parts, (z + step) % 4, 1), step))
    parts = held.astype(jnp.bfloat16)
    held = f32(pick(parts, y, 0))
    for step in (1, 2, 3):
        held = held + f32(along_y(pick(parts, (y + step) % 4, 0), step))
    mine = held.astype(jnp.bfloat16)
    held = f32(mine)
    for step in (1, 2, 3):
        held = held + f32(along_comm(mine, step))
    return held * factor


def local(feats, tiles, tile_src, tile_count, request, z_old, dual, target, w_rows, rho, beta):
    comms, nodes, width = feats.shape
    piece, hidden = w_rows.shape
    asks = [along_comm(request, rel) for rel in (1, 2, 3)]
    of_z, *asks = lax.optimization_barrier((weight_of_z(w_rows), *asks))
    chosen = call_choose(asks, feats)
    tiles, of_z, *chosen = lax.optimization_barrier((tiles, of_z, *chosen))
    heads = [along_comm(chosen[2 * n], 3 - n) for n in range(3)]
    near, far_off = [heads[0], heads[2]], [heads[1]]
    last1, last3, *near = lax.optimization_barrier((chosen[1], chosen[5], *near))
    last2, *far_off = lax.optimization_barrier((chosen[3], *far_off))
    heads = near[0], far_off[0], near[1]
    blocks = [along_comm(block, 3 - n) for n, block in enumerate((last1, last2, last3))]
    flat = lambda x: x.reshape(comms * nodes, hidden)
    acc, far, zs, ds, ts = call_own_products(
        tile_src, tile_count, request, feats, tiles, flat(z_old), flat(dual), flat(target)
    )
    weight = whole_weight(of_z)
    acc = call_head_products(tile_src, tile_count, far, heads, acc)
    new_z, new_dual, keep, send = call_update(
        tile_src, tile_count, far, blocks, acc, weight, zs, ds, ts, rho, beta, piece
    )
    total_nodes = comms * nodes * lax.axis_size("comm") * lax.axis_size("wide")
    grad = reduced(keep, send, 1.0 / math.sqrt(total_nodes))
    return new_z.reshape(z_old.shape), new_dual.reshape(z_old.shape), grad


def solution(mesh):
    split = P(("comm", "wide"))
    in_specs = (split,) * 8 + (P("wide"), P(), P())
    out_specs = (split, split, P("wide"))
    return jax.shard_map(local, mesh=mesh, in_specs=in_specs, out_specs=out_specs, check_vma=False)
```

```python
import functools
import math

import jax
import jax.numpy as jnp
from jax import lax
from jax.experimental import pallas as pl
from jax.experimental.pallas import tpu as pltpu
from jax.sharding import PartitionSpec as P

ROWS = 768
COLS = 256
FEATS = 768
EARLY = 128
CUT = 512
SMALL = pl.CostEstimate(flops=2**20, bytes_accessed=2**16, transcendentals=0)
SMEM = pl.BlockSpec(memory_space=pltpu.SMEM)
VMEM = pl.BlockSpec(memory_space=pltpu.VMEM)
HBM = pl.BlockSpec(memory_space=pltpu.HBM)


def shifted(x, axis, to):
    size = lax.axis_size(axis)
    return lax.ppermute(x, axis, [(i, to(i)) for i in range(size)])


def place(w):
    return w // 8, w // 2 % 4, w % 2


def along_comm(x, step):
    return shifted(x, "comm", lambda i: (i + step) % 4)


def along_core(x):
    return shifted(x, "wide", lambda w: w ^ 1)


def along_z(x, step):
    return shifted(x, "wide", lambda w: w // 8 * 8 + (w // 2 % 4 + step) % 4 * 2 + w % 2)


def along_y(x, step):
    return shifted(x, "wide", lambda w: (w // 8 + step) % 4 * 8 + w % 8)


def in_hbm(x):
    return pltpu.with_memory_space_constraint(x, pltpu.HBM)


def me_on_comm():
    return lax.axis_index("comm")


def pieces(width):
    return [(start, CUT, width) for start in (0, EARLY, 0)]


def choose(ask1, ask2, ask3, feats, *refs):
    outs, sems = refs[:-1], refs[-1]
    me = me_on_comm()
    copies = []
    for ask, bounds in zip((ask1, ask2, ask3), pieces(feats.shape[2])):
        for low, high in zip(bounds[:-1], bounds[1:]):
            n = len(copies)
            copies.append(
                pltpu.make_async_copy(feats.at[ask[0, me], :, low:high], outs[n], sems.at[n])
            )
    for c in copies:
        c.start()
    for c in copies:
        c.wait()


def call_choose(asks, feats):
    nodes, width = feats.shape[1:]
    shapes = [
        jax.ShapeDtypeStruct((nodes, high - low), feats.dtype)
        for bounds in pieces(width)
        for low, high in zip(bounds[:-1], bounds[1:])
    ]
    return pl.pallas_call(
        choose,
        out_shape=shapes,
        in_specs=[SMEM] * 3 + [HBM],
        out_specs=[VMEM] * len(shapes),
        scratch_shapes=[pltpu.SemaphoreType.DMA((len(shapes),))],
        compiler_params=pltpu.CompilerParams(vmem_limit_bytes=4 * 2**20),
        cost_estimate=SMALL,
        name="choose",
    )(*asks, in_hbm(feats))


def own_products(
    src, count, request, feats, tiles, z_old, dual, target,
    acc, far, zs, ds, ts, buf, sems, fsems, xsems,
):
    me = me_on_comm()
    comms, slots = tiles.shape[0], tiles.shape[1]
    local = feats.shape[0]

    def live(k, t):
        return t < count[k]

    def own(k, t):
        source = src[k, t]
        return (source < local) | (source == local + me)

    def near_copy(k, t):
        return pltpu.make_async_copy(tiles.at[k, t], buf.at[k, t], sems.at[k, t])

    def far_copy(k, t):
        return pltpu.make_async_copy(tiles.at[k, t], far.at[k, t], fsems.at[k, t])

    staged = [
        pltpu.make_async_copy(a, b, xsems.at[n])
        for n, (a, b) in enumerate(((z_old, zs), (dual, ds), (target, ts)))
    ]
    for k in range(comms):
        for t in range(slots):
            pl.when(live(k, t) & own(k, t))(near_copy(k, t).start)
    for k in range(comms):
        for t in range(slots):
            pl.when(live(k, t) & ~own(k, t))(far_copy(k, t).start)
    for c in staged:
        c.start()
    for k in range(comms):
        acc[k] = jnp.zeros(acc.shape[1:], jnp.float32)
        for t in range(slots):

            @pl.when(live(k, t) & own(k, t))
            def _():
                near_copy(k, t).wait()
                source = src[k, t]
                block = jnp.where(source < local, source, request[0, me])

                @pl.loop(0, acc.shape[1] // ROWS)
                def _(i):
                    rows = pl.ds(pl.multiple_of(i * ROWS, ROWS), ROWS)
                    acc[k, rows, :] += jnp.dot(
                        buf[k, t, rows, :], feats[block], preferred_element_type=jnp.float32
                    )

    for k in range(comms):
        for t in range(slots):
            pl.when(live(k, t) & ~own(k, t))(far_copy(k, t).wait)
    for c in staged:
        c.wait()


def call_own_products(src, count, request, feats, tiles, z_old, dual, target):
    comms, slots, nodes, _ = tiles.shape
    width = feats.shape[2]
    like = lambda a: jax.ShapeDtypeStruct(a.shape, a.dtype)
    return pl.pallas_call(
        own_products,
        out_shape=(
            jax.ShapeDtypeStruct((comms, nodes, width), jnp.float32),
            like(tiles), like(z_old), like(dual), like(target),
        ),
        in_specs=[SMEM, SMEM, SMEM, VMEM] + [HBM] * 4,
        out_specs=(VMEM,) * 5,
        scratch_shapes=[
            pltpu.VMEM(tiles.shape, tiles.dtype),
            pltpu.SemaphoreType.DMA((comms, slots)),
            pltpu.SemaphoreType.DMA((comms, slots)),
            pltpu.SemaphoreType.DMA((3,)),
        ],
        compiler_params=pltpu.CompilerParams(vmem_limit_bytes=16 * 2**20),
        cost_estimate=SMALL,
        name="own_products",
    )(src, count, request, feats, *map(in_hbm, (tiles, z_old, dual, target)))


def relation(src, count, k, t, local):
    rel = lax.rem(src[k, t] - local - me_on_comm() + 8, 4)
    return (t < count[k]) & (src[k, t] >= local) & (rel > 0), rel


def head_products(src, count, request, far, early, head1, head2, head3, before, acc):
    comms, slots, _, _ = far.shape
    opposite = request[0, lax.rem(me_on_comm() + 2, 4)]

    def add(k, t, low, block):
        acc[k, :, low:low + block.shape[1]] += jnp.dot(
            far[k, t], block, preferred_element_type=jnp.float32
        )

    for k in range(comms):
        for t in range(slots):
            live, rel = relation(src, count, k, t, comms)

            @pl.when(live & (rel == 1))
            def _():
                add(k, t, 0, head1[...])

            @pl.when(live & (rel == 2))
            def _():
                add(k, t, 0, early[opposite])
                add(k, t, EARLY, head2[...])

            @pl.when(live & (rel == 3))
            def _():
                add(k, t, 0, head3[...])


def call_head_products(src, count, request, far, early, heads, acc):
    return pl.pallas_call(
        head_products,
        out_shape=jax.ShapeDtypeStruct(acc.shape, acc.dtype),
        in_specs=[SMEM] * 3 + [VMEM] * 6,
        out_specs=VMEM,
        input_output_aliases={8: 0},
        compiler_params=pltpu.CompilerParams(vmem_limit_bytes=8 * 2**20),
        cost_estimate=SMALL,
        name="head_products",
    )(src, count, request, far, early, *heads, acc)


def update(
    src, count, far, from1, from2, from3, acc, weight, z_old, dual, target, rho, beta,
    new_z, new_dual, keep, send, agg, total, zbuf, dbuf, osems,
):
    core = my_core()
    comms, slots, nodes, _ = far.shape
    width, hidden = weight.shape
    per = nodes // ROWS
    steps = comms * per

    def out_copies(i):
        rows = pl.ds(pl.multiple_of(i * ROWS, ROWS), ROWS)
        return (
            pltpu.make_async_copy(zbuf.at[rows, :], new_z.at[rows, :], osems.at[0, i]),
            pltpu.make_async_copy(dbuf.at[rows, :], new_dual.at[rows, :], osems.at[1, i]),
        )

    @pl.loop(0, steps)
    def _(i):
        k = i // per
        rows = pl.ds(pl.multiple_of((i - k * per) * ROWS, ROWS), ROWS)
        flat = pl.ds(pl.multiple_of(i * ROWS, ROWS), ROWS)
        total[...] = acc[k, rows, :]
        for t in range(slots):
            live, rel = relation(src, count, k, t, comms)
            for r, block in enumerate((from1, from2, from3), 1):

                @pl.when(live & (rel == r))
                def _():
                    total[:, CUT:] += jnp.dot(
                        far[k, t, rows, :], block[...], preferred_element_type=jnp.float32
                    )

        part = total[...].astype(jnp.bfloat16)
        agg[flat, :] = part
        for h in range(hidden // COLS):
            cols = slice(h * COLS, (h + 1) * COLS)
            r, b = rho[:, cols], beta[:, cols]
            share = b / (r + b)
            pre = jnp.dot(part, weight[:, cols], preferred_element_type=jnp.float32)
            v = pre + dual[flat, cols].astype(jnp.float32) * (1.0 / r)
            gap = jnp.where(
                z_old[flat, cols].astype(jnp.float32) > 0,
                (v - target[flat, cols].astype(jnp.float32)) * share,
                0.0,
            )
            zbuf[flat, cols] = (v - gap).astype(jnp.bfloat16)
            dbuf[flat, cols] = (r * gap).astype(jnp.bfloat16)
        for c in out_copies(i):
            c.start()

    piece = keep.shape[1]
    group = FEATS // piece

    for f in range(width // FEATS):
        grad = lax.dot_general(
            agg[:, f * FEATS:(f + 1) * FEATS], dbuf[...],
            (((0,), (0,)), ((), ())), preferred_element_type=jnp.float32,
        ).astype(jnp.bfloat16)
        for n in range(group):
            at = f * group + n
            rows = grad[n * piece:(n + 1) * piece]

            @pl.when(core == at % 2)
            def _():
                keep[at // 2] = rows

            @pl.when(core != at % 2)
            def _():
                send[at // 2] = rows

    @pl.loop(0, steps)
    def _(i):
        for c in out_copies(i):
            c.wait()


def call_update(src, count, far, blocks, acc, weight, z_old, dual, target, rho, beta, piece):
    comms, slots, nodes, _ = far.shape
    width, hidden = weight.shape
    flat = comms * nodes
    steps = flat // ROWS
    wide = jax.ShapeDtypeStruct((flat, hidden), jnp.bfloat16)
    half = jax.ShapeDtypeStruct((width // piece // 2, piece, hidden), jnp.bfloat16)
    return pl.pallas_call(
        update,
        out_shape=(wide, wide, half, half),
        in_specs=[SMEM, SMEM] + [VMEM] * 11,
        out_specs=(HBM, HBM, VMEM, VMEM),
        scratch_shapes=[
            pltpu.VMEM((flat, width), jnp.bfloat16),
            pltpu.VMEM((ROWS, width), jnp.float32),
            pltpu.VMEM((flat, hidden), jnp.bfloat16),
            pltpu.VMEM((flat, hidden), jnp.bfloat16),
            pltpu.SemaphoreType.DMA((2, steps)),
        ],
        compiler_params=pltpu.CompilerParams(vmem_limit_bytes=24 * 2**20),
        cost_estimate=pl.CostEstimate(
            flops=4 * flat * width * hidden + 3 * 2 * nodes * nodes * width,
            bytes_accessed=6 * 2**20,
            transcendentals=0,
        ),
        name="update",
    )(src, count, far, *blocks, acc, weight, z_old, dual, target, rho[None], beta[None])


def arrange(first, *refs):
    out = refs[-1]
    for d, part in enumerate(refs[:-1]):
        out[lax.rem(first() + d, len(refs) - 1)] = part[...]


def call_arrange(first, parts, name):
    shape = jax.ShapeDtypeStruct((len(parts), *parts[0].shape), parts[0].dtype)
    return pl.pallas_call(
        functools.partial(arrange, first),
        out_shape=shape,
        in_specs=[VMEM] * len(parts),
        out_specs=VMEM,
        compiler_params=pltpu.CompilerParams(vmem_limit_bytes=4 * 2**20),
        cost_estimate=SMALL,
        name=name,
    )(*parts)


def my_y():
    return lax.axis_index("wide") // 8


def my_z():
    return lax.rem(lax.axis_index("wide") // 2, 4)


def my_core():
    return lax.rem(lax.axis_index("wide"), 2)


def pair(mine, other, out):
    core = my_core()

    @pl.loop(0, mine.shape[0])
    def _(i):
        out[i, core] = mine[i]
        out[i, 1 - core] = other[i]


def call_pair(mine, other):
    groups, piece, hidden = mine.shape
    return pl.pallas_call(
        pair,
        out_shape=jax.ShapeDtypeStruct((groups, 2, piece, hidden), mine.dtype),
        in_specs=[VMEM, VMEM],
        out_specs=VMEM,
        compiler_params=pltpu.CompilerParams(vmem_limit_bytes=4 * 2**20),
        cost_estimate=SMALL,
        name="pair_rows",
    )(mine, other)


def weight_of_z(rows):
    return call_arrange(my_z, [rows] + [along_z(rows, 4 - d) for d in (1, 2, 3)], "rows_of_z")


def whole_weight(parts, after):
    piece, hidden = parts.shape[1:]
    rows = [parts] + [along_y(parts, 4 - d) for d in (1, 2, 3)]
    after, *rows = lax.optimization_barrier((after, *rows))
    parts = call_arrange(my_y, rows, "rows_of_y").reshape(16, piece, hidden)
    return call_pair(parts, along_core(parts)).reshape(32 * piece, hidden), after


def reduced(keep, send, factor):
    y, z, _ = place(lax.axis_index("wide"))
    pick = functools.partial(lax.dynamic_index_in_dim, keepdims=False)
    f32 = lambda x: x.astype(jnp.float32)
    parts = (f32(keep) + f32(along_core(send))).astype(jnp.bfloat16)
    parts = parts.reshape(4, 4, *keep.shape[1:])
    held = f32(pick(parts, z, 1))
    for step in (1, 2, 3):
        held = held + f32(along_z(pick(parts, (z + step) % 4, 1), step))
    parts = held.astype(jnp.bfloat16)
    held = f32(pick(parts, y, 0))
    for step in (1, 2, 3):
        held = held + f32(along_y(pick(parts, (y + step) % 4, 0), step))
    mine = held.astype(jnp.bfloat16)
    held = f32(mine)
    for step in (1, 2, 3):
        held = held + f32(along_comm(mine, step))
    return held * factor


def local(feats, tiles, tile_src, tile_count, request, z_old, dual, target, w_rows, rho, beta):
    comms, nodes, width = feats.shape
    piece, hidden = w_rows.shape
    asks = [along_comm(request, rel) for rel in (1, 2, 3)]
    first, w_rows, *asks = lax.optimization_barrier((feats[:, :, :EARLY], w_rows, *asks))
    early = along_comm(first, 2)
    of_z, *asks = lax.optimization_barrier((weight_of_z(w_rows), *asks))
    chosen = call_choose(asks, feats)
    tiles, of_z, *chosen = lax.optimization_barrier((tiles, of_z, *chosen))
    early, chosen[2] = lax.optimization_barrier((early, chosen[2]))
    heads = [along_comm(chosen[2 * n], 3 - n) for n in range(3)]
    near, far_off = [heads[0], heads[2]], [heads[1]]
    last1, last3, *near = lax.optimization_barrier((chosen[1], chosen[5], *near))
    last2, *far_off = lax.optimization_barrier((chosen[3], *far_off))
    heads = near[0], far_off[0], near[1]
    blocks = [along_comm(block, 3 - n) for n, block in enumerate((last1, last2, last3))]
    flat = lambda x: x.reshape(comms * nodes, hidden)
    acc, far, zs, ds, ts = call_own_products(
        tile_src, tile_count, request, feats, tiles, flat(z_old), flat(dual), flat(target)
    )
    weight, acc = whole_weight(of_z, acc)
    acc = call_head_products(tile_src, tile_count, request, far, early, heads, acc)
    new_z, new_dual, keep, send = call_update(
        tile_src, tile_count, far, blocks, acc, weight, zs, ds, ts, rho, beta, piece
    )
    total_nodes = comms * nodes * lax.axis_size("comm") * lax.axis_size("wide")
    grad = reduced(keep, send, 1.0 / math.sqrt(total_nodes))
    return new_z.reshape(z_old.shape), new_dual.reshape(z_old.shape), grad


def solution(mesh):
    split = P(("comm", "wide"))
    in_specs = (split,) * 8 + (P("wide"), P(), P())
    out_specs = (split, split, P("wide"))
    return jax.shard_map(local, mesh=mesh, in_specs=in_specs, out_specs=out_specs, check_vma=False)
```

```python
import functools
import math

import jax
import jax.numpy as jnp
from jax import lax
from jax.experimental import pallas as pl
from jax.experimental.pallas import tpu as pltpu
from jax.sharding import PartitionSpec as P

ROWS = 768
COLS = 256
FEATS = 768
EARLY = 128
CUT = 512
SMALL = pl.CostEstimate(flops=2**20, bytes_accessed=2**16, transcendentals=0)
SMEM = pl.BlockSpec(memory_space=pltpu.SMEM)
VMEM = pl.BlockSpec(memory_space=pltpu.VMEM)
HBM = pl.BlockSpec(memory_space=pltpu.HBM)


def shifted(x, axis, to):
    size = lax.axis_size(axis)
    return lax.ppermute(x, axis, [(i, to(i)) for i in range(size)])


def place(w):
    return w // 8, w // 2 % 4, w % 2


def along_comm(x, step):
    return shifted(x, "comm", lambda i: (i + step) % 4)


def along_core(x):
    return shifted(x, "wide", lambda w: w ^ 1)


def along_z(x, step):
    return shifted(x, "wide", lambda w: w // 8 * 8 + (w // 2 % 4 + step) % 4 * 2 + w % 2)


def along_y(x, step):
    return shifted(x, "wide", lambda w: (w // 8 + step) % 4 * 8 + w % 8)


def in_hbm(x):
    return pltpu.with_memory_space_constraint(x, pltpu.HBM)


def me_on_comm():
    return lax.axis_index("comm")


def pieces(width):
    return [(start, CUT, width) for start in (0, EARLY, 0)]


def choose(ask1, ask2, ask3, feats, *refs):
    outs, sems = refs[:-1], refs[-1]
    me = me_on_comm()
    copies = []
    for ask, bounds in zip((ask1, ask2, ask3), pieces(feats.shape[2])):
        for low, high in zip(bounds[:-1], bounds[1:]):
            n = len(copies)
            copies.append(
                pltpu.make_async_copy(feats.at[ask[0, me], :, low:high], outs[n], sems.at[n])
            )
    for c in copies:
        c.start()
    for c in copies:
        c.wait()


def call_choose(asks, feats):
    nodes, width = feats.shape[1:]
    shapes = [
        jax.ShapeDtypeStruct((nodes, high - low), feats.dtype)
        for bounds in pieces(width)
        for low, high in zip(bounds[:-1], bounds[1:])
    ]
    return pl.pallas_call(
        choose,
        out_shape=shapes,
        in_specs=[SMEM] * 3 + [HBM],
        out_specs=[VMEM] * len(shapes),
        scratch_shapes=[pltpu.SemaphoreType.DMA((len(shapes),))],
        compiler_params=pltpu.CompilerParams(vmem_limit_bytes=4 * 2**20),
        cost_estimate=SMALL,
        name="choose",
    )(*asks, in_hbm(feats))


def own_products(
    src, count, request, feats, tiles, z_old, dual, target,
    acc, far, zs, ds, ts, buf, sems, fsems, xsems,
):
    me = me_on_comm()
    comms, slots = tiles.shape[0], tiles.shape[1]
    local = feats.shape[0]

    def live(k, t):
        return t < count[k]

    def own(k, t):
        source = src[k, t]
        return (source < local) | (source == local + me)

    def near_copy(k, t):
        return pltpu.make_async_copy(tiles.at[k, t], buf.at[k, t], sems.at[k, t])

    def far_copy(k, t):
        return pltpu.make_async_copy(tiles.at[k, t], far.at[k, t], fsems.at[k, t])

    staged = [
        pltpu.make_async_copy(a, b, xsems.at[n])
        for n, (a, b) in enumerate(((z_old, zs), (dual, ds), (target, ts)))
    ]
    for k in range(comms):
        for t in range(slots):
            pl.when(live(k, t) & own(k, t))(near_copy(k, t).start)
    for k in range(comms):
        for t in range(slots):
            pl.when(live(k, t) & ~own(k, t))(far_copy(k, t).start)
    for c in staged:
        c.start()
    for k in range(comms):
        acc[k] = jnp.zeros(acc.shape[1:], jnp.float32)
        for t in range(slots):

            @pl.when(live(k, t) & own(k, t))
            def _():
                near_copy(k, t).wait()
                source = src[k, t]
                block = jnp.where(source < local, source, request[0, me])

                @pl.loop(0, acc.shape[1] // ROWS)
                def _(i):
                    rows = pl.ds(pl.multiple_of(i * ROWS, ROWS), ROWS)
                    acc[k, rows, :] += jnp.dot(
                        buf[k, t, rows, :], feats[block], preferred_element_type=jnp.float32
                    )

    for k in range(comms):
        for t in range(slots):
            pl.when(live(k, t) & ~own(k, t))(far_copy(k, t).wait)
    for c in staged:
        c.wait()


def call_own_products(src, count, request, feats, tiles, z_old, dual, target):
    comms, slots, nodes, _ = tiles.shape
    width = feats.shape[2]
    like = lambda a: jax.ShapeDtypeStruct(a.shape, a.dtype)
    return pl.pallas_call(
        own_products,
        out_shape=(
            jax.ShapeDtypeStruct((comms, nodes, width), jnp.float32),
            like(tiles), like(z_old), like(dual), like(target),
        ),
        in_specs=[SMEM, SMEM, SMEM, VMEM] + [HBM] * 4,
        out_specs=(VMEM,) * 5,
        scratch_shapes=[
            pltpu.VMEM(tiles.shape, tiles.dtype),
            pltpu.SemaphoreType.DMA((comms, slots)),
            pltpu.SemaphoreType.DMA((comms, slots)),
            pltpu.SemaphoreType.DMA((3,)),
        ],
        compiler_params=pltpu.CompilerParams(vmem_limit_bytes=16 * 2**20),
        cost_estimate=SMALL,
        name="own_products",
    )(src, count, request, feats, *map(in_hbm, (tiles, z_old, dual, target)))


def relation(src, count, k, t, local):
    rel = lax.rem(src[k, t] - local - me_on_comm() + 8, 4)
    return (t < count[k]) & (src[k, t] >= local) & (rel > 0), rel


def head_products(src, count, request, far, early, head1, head2, head3, before, acc):
    comms, slots, _, _ = far.shape
    opposite = request[0, lax.rem(me_on_comm() + 2, 4)]

    def add(k, t, low, block):
        acc[k, :, low:low + block.shape[1]] += jnp.dot(
            far[k, t], block, preferred_element_type=jnp.float32
        )

    for k in range(comms):
        for t in range(slots):
            live, rel = relation(src, count, k, t, comms)

            @pl.when(live & (rel == 1))
            def _():
                add(k, t, 0, head1[...])

            @pl.when(live & (rel == 2))
            def _():
                add(k, t, 0, early[opposite])
                add(k, t, EARLY, head2[...])

            @pl.when(live & (rel == 3))
            def _():
                add(k, t, 0, head3[...])


def call_head_products(src, count, request, far, early, heads, acc):
    return pl.pallas_call(
        head_products,
        out_shape=jax.ShapeDtypeStruct(acc.shape, acc.dtype),
        in_specs=[SMEM] * 3 + [VMEM] * 6,
        out_specs=VMEM,
        input_output_aliases={8: 0},
        compiler_params=pltpu.CompilerParams(vmem_limit_bytes=8 * 2**20),
        cost_estimate=SMALL,
        name="head_products",
    )(src, count, request, far, early, *heads, acc)


def update(
    src, count, far, from1, from2, from3, acc, weight, z_old, dual, target, rho, beta,
    new_z, new_dual, keep, send, agg, total, zbuf, dbuf, osems,
):
    core = my_core()
    comms, slots, nodes, _ = far.shape
    width, hidden = weight.shape
    per = nodes // ROWS
    steps = comms * per

    def out_copies(i):
        rows = pl.ds(pl.multiple_of(i * ROWS, ROWS), ROWS)
        return (
            pltpu.make_async_copy(zbuf.at[rows, :], new_z.at[rows, :], osems.at[0, i]),
            pltpu.make_async_copy(dbuf.at[rows, :], new_dual.at[rows, :], osems.at[1, i]),
        )

    @pl.loop(0, steps)
    def _(i):
        k = i // per
        rows = pl.ds(pl.multiple_of((i - k * per) * ROWS, ROWS), ROWS)
        flat = pl.ds(pl.multiple_of(i * ROWS, ROWS), ROWS)
        total[...] = acc[k, rows, :]
        for t in range(slots):
            live, rel = relation(src, count, k, t, comms)
            for r, block in enumerate((from1, from2, from3), 1):

                @pl.when(live & (rel == r))
                def _():
                    total[:, CUT:] += jnp.dot(
                        far[k, t, rows, :], block[...], preferred_element_type=jnp.float32
                    )

        part = total[...].astype(jnp.bfloat16)
        agg[flat, :] = part
        for h in range(hidden // COLS):
            cols = slice(h * COLS, (h + 1) * COLS)
            r, b = rho[:, cols], beta[:, cols]
            share = b / (r + b)
            pre = jnp.dot(part, weight[:, cols], preferred_element_type=jnp.float32)
            v = pre + dual[flat, cols].astype(jnp.float32) * (1.0 / r)
            gap = jnp.where(
                z_old[flat, cols].astype(jnp.float32) > 0,
                (v - target[flat, cols].astype(jnp.float32)) * share,
                0.0,
            )
            zbuf[flat, cols] = (v - gap).astype(jnp.bfloat16)
            dbuf[flat, cols] = (r * gap).astype(jnp.bfloat16)
        for c in out_copies(i):
            c.start()

    piece = keep.shape[1]
    group = FEATS // piece

    for f in range(width // FEATS):
        grad = lax.dot_general(
            agg[:, f * FEATS:(f + 1) * FEATS], dbuf[...],
            (((0,), (0,)), ((), ())), preferred_element_type=jnp.float32,
        ).astype(jnp.bfloat16)
        for n in range(group):
            at = f * group + n
            rows = grad[n * piece:(n + 1) * piece]

            @pl.when(core == at % 2)
            def _():
                keep[at // 2] = rows

            @pl.when(core != at % 2)
            def _():
                send[at // 2] = rows

    @pl.loop(0, steps)
    def _(i):
        for c in out_copies(i):
            c.wait()


def call_update(src, count, far, blocks, acc, weight, z_old, dual, target, rho, beta, piece):
    comms, slots, nodes, _ = far.shape
    width, hidden = weight.shape
    flat = comms * nodes
    steps = flat // ROWS
    wide = jax.ShapeDtypeStruct((flat, hidden), jnp.bfloat16)
    half = jax.ShapeDtypeStruct((width // piece // 2, piece, hidden), jnp.bfloat16)
    return pl.pallas_call(
        update,
        out_shape=(wide, wide, half, half),
        in_specs=[SMEM, SMEM] + [VMEM] * 11,
        out_specs=(HBM, HBM, VMEM, VMEM),
        scratch_shapes=[
            pltpu.VMEM((flat, width), jnp.bfloat16),
            pltpu.VMEM((ROWS, width), jnp.float32),
            pltpu.VMEM((flat, hidden), jnp.bfloat16),
            pltpu.VMEM((flat, hidden), jnp.bfloat16),
            pltpu.SemaphoreType.DMA((2, steps)),
        ],
        compiler_params=pltpu.CompilerParams(vmem_limit_bytes=24 * 2**20),
        cost_estimate=pl.CostEstimate(
            flops=4 * flat * width * hidden + 3 * 2 * nodes * nodes * width,
            bytes_accessed=6 * 2**20,
            transcendentals=0,
        ),
        name="update",
    )(src, count, far, *blocks, acc, weight, z_old, dual, target, rho[None], beta[None])


def arrange(first, *refs):
    out = refs[-1]
    for d, part in enumerate(refs[:-1]):
        out[lax.rem(first() + d, len(refs) - 1)] = part[...]


def call_arrange(first, parts, name):
    shape = jax.ShapeDtypeStruct((len(parts), *parts[0].shape), parts[0].dtype)
    return pl.pallas_call(
        functools.partial(arrange, first),
        out_shape=shape,
        in_specs=[VMEM] * len(parts),
        out_specs=VMEM,
        compiler_params=pltpu.CompilerParams(vmem_limit_bytes=4 * 2**20),
        cost_estimate=SMALL,
        name=name,
    )(*parts)


def my_y():
    return lax.axis_index("wide") // 8


def my_z():
    return lax.rem(lax.axis_index("wide") // 2, 4)


def my_core():
    return lax.rem(lax.axis_index("wide"), 2)


def pair(mine, other, out):
    core = my_core()

    @pl.loop(0, mine.shape[0])
    def _(i):
        out[i, core] = mine[i]
        out[i, 1 - core] = other[i]


def call_pair(mine, other):
    groups, piece, hidden = mine.shape
    return pl.pallas_call(
        pair,
        out_shape=jax.ShapeDtypeStruct((groups, 2, piece, hidden), mine.dtype),
        in_specs=[VMEM, VMEM],
        out_specs=VMEM,
        compiler_params=pltpu.CompilerParams(vmem_limit_bytes=4 * 2**20),
        cost_estimate=SMALL,
        name="pair_rows",
    )(mine, other)


def whole_weight(parts, after):
    piece, hidden = parts.shape[1:]
    rows = [parts] + [along_y(parts, 4 - d) for d in (1, 2, 3)]
    after, *rows = lax.optimization_barrier((after, *rows))
    parts = call_arrange(my_y, rows, "rows_of_y").reshape(16, piece, hidden)
    return call_pair(parts, along_core(parts)).reshape(32 * piece, hidden), after


def reduced(keep, send, factor):
    y, z, _ = place(lax.axis_index("wide"))
    pick = functools.partial(lax.dynamic_index_in_dim, keepdims=False)
    f32 = lambda x: x.astype(jnp.float32)
    parts = (f32(keep) + f32(along_core(send))).astype(jnp.bfloat16)
    parts = parts.reshape(4, 4, *keep.shape[1:])
    held = f32(pick(parts, z, 1))
    for step in (1, 2, 3):
        held = held + f32(along_z(pick(parts, (z + step) % 4, 1), step))
    parts = held.astype(jnp.bfloat16)
    held = f32(pick(parts, y, 0))
    for step in (1, 2, 3):
        held = held + f32(along_y(pick(parts, (y + step) % 4, 0), step))
    mine = held.astype(jnp.bfloat16)
    held = f32(mine)
    for step in (1, 2, 3):
        held = held + f32(along_comm(mine, step))
    return held * factor


def local(feats, tiles, tile_src, tile_count, request, z_old, dual, target, w_rows, rho, beta):
    comms, nodes, width = feats.shape
    piece, hidden = w_rows.shape
    asks = [along_comm(request, rel) for rel in (1, 2, 3)]
    first, w_rows, *asks = lax.optimization_barrier((feats[:, :, :EARLY], w_rows, *asks))
    early = along_comm(first, 2)
    beside = [along_z(w_rows, 4 - d) for d in (1, 2, 3)]
    chosen = call_choose(asks, feats)
    tiles, *both = lax.optimization_barrier((tiles, *beside, *chosen))
    beside, chosen = both[:3], both[3:]
    of_z = call_arrange(my_z, [w_rows, *beside], "rows_of_z")
    early, chosen[2] = lax.optimization_barrier((early, chosen[2]))
    heads = [along_comm(chosen[2 * n], 3 - n) for n in range(3)]
    near, far_off = [heads[0], heads[2]], [heads[1]]
    last1, last3, *near = lax.optimization_barrier((chosen[1], chosen[5], *near))
    last2, *far_off = lax.optimization_barrier((chosen[3], *far_off))
    heads = near[0], far_off[0], near[1]
    blocks = [along_comm(block, 3 - n) for n, block in enumerate((last1, last2, last3))]
    flat = lambda x: x.reshape(comms * nodes, hidden)
    acc, far, zs, ds, ts = call_own_products(
        tile_src, tile_count, request, feats, tiles, flat(z_old), flat(dual), flat(target)
    )
    weight, acc = whole_weight(of_z, acc)
    acc = call_head_products(tile_src, tile_count, request, far, early, heads, acc)
    new_z, new_dual, keep, send = call_update(
        tile_src, tile_count, far, blocks, acc, weight, zs, ds, ts, rho, beta, piece
    )
    total_nodes = comms * nodes * lax.axis_size("comm") * lax.axis_size("wide")
    grad = reduced(keep, send, 1.0 / math.sqrt(total_nodes))
    return new_z.reshape(z_old.shape), new_dual.reshape(z_old.shape), grad


def solution(mesh):
    split = P(("comm", "wide"))
    in_specs = (split,) * 8 + (P("wide"), P(), P())
    out_specs = (split, split, P("wide"))
    return jax.shard_map(local, mesh=mesh, in_specs=in_specs, out_specs=out_specs, check_vma=False)
```

```python
import functools
import math

import jax
import jax.numpy as jnp
from jax import lax
from jax.experimental import pallas as pl
from jax.experimental.pallas import tpu as pltpu
from jax.sharding import PartitionSpec as P

ROWS = 768
COLS = 256
FEATS = 768
EARLY = 128
CUT = 512
SMALL = pl.CostEstimate(flops=2**20, bytes_accessed=2**16, transcendentals=0)
SMEM = pl.BlockSpec(memory_space=pltpu.SMEM)
VMEM = pl.BlockSpec(memory_space=pltpu.VMEM)
HBM = pl.BlockSpec(memory_space=pltpu.HBM)


def shifted(x, axis, to):
    size = lax.axis_size(axis)
    return lax.ppermute(x, axis, [(i, to(i)) for i in range(size)])


def place(w):
    return w // 8, w // 2 % 4, w % 2


def along_comm(x, step):
    return shifted(x, "comm", lambda i: (i + step) % 4)


def along_core(x):
    return shifted(x, "wide", lambda w: w ^ 1)


def along_z(x, step):
    return shifted(x, "wide", lambda w: w // 8 * 8 + (w // 2 % 4 + step) % 4 * 2 + w % 2)


def along_y(x, step):
    return shifted(x, "wide", lambda w: (w // 8 + step) % 4 * 8 + w % 8)


def in_hbm(x):
    return pltpu.with_memory_space_constraint(x, pltpu.HBM)


def me_on_comm():
    return lax.axis_index("comm")


def pieces(width):
    return [(start, CUT, width) for start in (0, EARLY, 0)]


def choose(ask1, ask2, ask3, feats, *refs):
    outs, sems = refs[:-1], refs[-1]
    me = me_on_comm()
    copies = []
    for ask, bounds in zip((ask1, ask2, ask3), pieces(feats.shape[2])):
        for low, high in zip(bounds[:-1], bounds[1:]):
            n = len(copies)
            copies.append(
                pltpu.make_async_copy(feats.at[ask[0, me], :, low:high], outs[n], sems.at[n])
            )
    for c in copies:
        c.start()
    for c in copies:
        c.wait()


def call_choose(asks, feats):
    nodes, width = feats.shape[1:]
    shapes = [
        jax.ShapeDtypeStruct((nodes, high - low), feats.dtype)
        for bounds in pieces(width)
        for low, high in zip(bounds[:-1], bounds[1:])
    ]
    return pl.pallas_call(
        choose,
        out_shape=shapes,
        in_specs=[SMEM] * 3 + [HBM],
        out_specs=[VMEM] * len(shapes),
        scratch_shapes=[pltpu.SemaphoreType.DMA((len(shapes),))],
        compiler_params=pltpu.CompilerParams(vmem_limit_bytes=4 * 2**20),
        cost_estimate=SMALL,
        name="choose",
    )(*asks, in_hbm(feats))


def own_products(
    src, count, request, feats, tiles, z_old, dual, target,
    acc, far, zs, ds, ts, buf, sems, fsems, xsems,
):
    me = me_on_comm()
    comms, slots = tiles.shape[0], tiles.shape[1]
    local = feats.shape[0]

    def live(k, t):
        return t < count[k]

    def own(k, t):
        source = src[k, t]
        return (source < local) | (source == local + me)

    def near_copy(k, t):
        return pltpu.make_async_copy(tiles.at[k, t], buf.at[k, t], sems.at[k, t])

    def far_copy(k, t):
        return pltpu.make_async_copy(tiles.at[k, t], far.at[k, t], fsems.at[k, t])

    staged = [
        pltpu.make_async_copy(a, b, xsems.at[n])
        for n, (a, b) in enumerate(((z_old, zs), (dual, ds), (target, ts)))
    ]
    for k in range(comms):
        for t in range(slots):
            pl.when(live(k, t) & own(k, t))(near_copy(k, t).start)
    for k in range(comms):
        for t in range(slots):
            pl.when(live(k, t) & ~own(k, t))(far_copy(k, t).start)
    for c in staged:
        c.start()
    for k in range(comms):
        acc[k] = jnp.zeros(acc.shape[1:], jnp.float32)
        for t in range(slots):

            @pl.when(live(k, t) & own(k, t))
            def _():
                near_copy(k, t).wait()
                source = src[k, t]
                block = jnp.where(source < local, source, request[0, me])

                @pl.loop(0, acc.shape[1] // ROWS)
                def _(i):
                    rows = pl.ds(pl.multiple_of(i * ROWS, ROWS), ROWS)
                    acc[k, rows, :] += jnp.dot(
                        buf[k, t, rows, :], feats[block], preferred_element_type=jnp.float32
                    )

    for k in range(comms):
        for t in range(slots):
            pl.when(live(k, t) & ~own(k, t))(far_copy(k, t).wait)
    for c in staged:
        c.wait()


def call_own_products(src, count, request, feats, tiles, z_old, dual, target):
    comms, slots, nodes, _ = tiles.shape
    width = feats.shape[2]
    like = lambda a: jax.ShapeDtypeStruct(a.shape, a.dtype)
    return pl.pallas_call(
        own_products,
        out_shape=(
            jax.ShapeDtypeStruct((comms, nodes, width), jnp.float32),
            like(tiles), like(z_old), like(dual), like(target),
        ),
        in_specs=[SMEM, SMEM, SMEM, VMEM] + [HBM] * 4,
        out_specs=(VMEM,) * 5,
        scratch_shapes=[
            pltpu.VMEM(tiles.shape, tiles.dtype),
            pltpu.SemaphoreType.DMA((comms, slots)),
            pltpu.SemaphoreType.DMA((comms, slots)),
            pltpu.SemaphoreType.DMA((3,)),
        ],
        compiler_params=pltpu.CompilerParams(vmem_limit_bytes=16 * 2**20),
        cost_estimate=SMALL,
        name="own_products",
    )(src, count, request, feats, *map(in_hbm, (tiles, z_old, dual, target)))


def relation(src, count, k, t, local):
    rel = lax.rem(src[k, t] - local - me_on_comm() + 8, 4)
    return (t < count[k]) & (src[k, t] >= local) & (rel > 0), rel


def head_products(src, count, request, far, early, head1, head2, head3, before, acc):
    comms, slots, _, _ = far.shape
    opposite = request[0, lax.rem(me_on_comm() + 2, 4)]

    def add(k, t, low, block):
        acc[k, :, low:low + block.shape[1]] += jnp.dot(
            far[k, t], block, preferred_element_type=jnp.float32
        )

    for k in range(comms):
        for t in range(slots):
            live, rel = relation(src, count, k, t, comms)

            @pl.when(live & (rel == 1))
            def _():
                add(k, t, 0, head1[...])

            @pl.when(live & (rel == 2))
            def _():
                add(k, t, 0, early[opposite])
                add(k, t, EARLY, head2[...])

            @pl.when(live & (rel == 3))
            def _():
                add(k, t, 0, head3[...])


def call_head_products(src, count, request, far, early, heads, acc):
    return pl.pallas_call(
        head_products,
        out_shape=jax.ShapeDtypeStruct(acc.shape, acc.dtype),
        in_specs=[SMEM] * 3 + [VMEM] * 6,
        out_specs=VMEM,
        input_output_aliases={8: 0},
        compiler_params=pltpu.CompilerParams(vmem_limit_bytes=8 * 2**20),
        cost_estimate=SMALL,
        name="head_products",
    )(src, count, request, far, early, *heads, acc)


def update(
    src, count, far, from1, from2, from3, acc, weight, z_old, dual, target, rho, beta,
    new_z, new_dual, keep, send, agg, total, zbuf, dbuf, osems,
):
    core = my_core()
    comms, slots, nodes, _ = far.shape
    width, hidden = weight.shape
    per = nodes // ROWS
    steps = comms * per

    def out_copies(i):
        rows = pl.ds(pl.multiple_of(i * ROWS, ROWS), ROWS)
        return (
            pltpu.make_async_copy(zbuf.at[rows, :], new_z.at[rows, :], osems.at[0, i]),
            pltpu.make_async_copy(dbuf.at[rows, :], new_dual.at[rows, :], osems.at[1, i]),
        )

    @pl.loop(0, steps)
    def _(i):
        k = i // per
        rows = pl.ds(pl.multiple_of((i - k * per) * ROWS, ROWS), ROWS)
        flat = pl.ds(pl.multiple_of(i * ROWS, ROWS), ROWS)
        total[...] = acc[k, rows, :]
        for t in range(slots):
            live, rel = relation(src, count, k, t, comms)
            for r, block in enumerate((from1, from2, from3), 1):

                @pl.when(live & (rel == r))
                def _():
                    total[:, CUT:] += jnp.dot(
                        far[k, t, rows, :], block[...], preferred_element_type=jnp.float32
                    )

        part = total[...].astype(jnp.bfloat16)
        agg[flat, :] = part
        for h in range(hidden // COLS):
            cols = slice(h * COLS, (h + 1) * COLS)
            r, b = rho[:, cols], beta[:, cols]
            share = b / (r + b)
            pre = jnp.dot(part, weight[:, cols], preferred_element_type=jnp.float32)
            v = pre + dual[flat, cols].astype(jnp.float32) * (1.0 / r)
            gap = jnp.where(
                z_old[flat, cols].astype(jnp.float32) > 0,
                (v - target[flat, cols].astype(jnp.float32)) * share,
                0.0,
            )
            zbuf[flat, cols] = (v - gap).astype(jnp.bfloat16)
            dbuf[flat, cols] = (r * gap).astype(jnp.bfloat16)
        for c in out_copies(i):
            c.start()

    piece = keep.shape[1]
    group = FEATS // piece

    for f in range(width // FEATS):
        grad = lax.dot_general(
            agg[:, f * FEATS:(f + 1) * FEATS], dbuf[...],
            (((0,), (0,)), ((), ())), preferred_element_type=jnp.float32,
        ).astype(jnp.bfloat16)
        for n in range(group):
            at = f * group + n
            rows = grad[n * piece:(n + 1) * piece]

            @pl.when(core == at % 2)
            def _():
                keep[at // 2] = rows

            @pl.when(core != at % 2)
            def _():
                send[at // 2] = rows

    @pl.loop(0, steps)
    def _(i):
        for c in out_copies(i):
            c.wait()


def call_update(src, count, far, blocks, acc, weight, z_old, dual, target, rho, beta, piece):
    comms, slots, nodes, _ = far.shape
    width, hidden = weight.shape
    flat = comms * nodes
    steps = flat // ROWS
    wide = jax.ShapeDtypeStruct((flat, hidden), jnp.bfloat16)
    half = jax.ShapeDtypeStruct((width // piece // 2, piece, hidden), jnp.bfloat16)
    return pl.pallas_call(
        update,
        out_shape=(wide, wide, half, half),
        in_specs=[SMEM, SMEM] + [VMEM] * 11,
        out_specs=(HBM, HBM, VMEM, VMEM),
        scratch_shapes=[
            pltpu.VMEM((flat, width), jnp.bfloat16),
            pltpu.VMEM((ROWS, width), jnp.float32),
            pltpu.VMEM((flat, hidden), jnp.bfloat16),
            pltpu.VMEM((flat, hidden), jnp.bfloat16),
            pltpu.SemaphoreType.DMA((2, steps)),
        ],
        compiler_params=pltpu.CompilerParams(vmem_limit_bytes=24 * 2**20),
        cost_estimate=pl.CostEstimate(
            flops=4 * flat * width * hidden + 3 * 2 * nodes * nodes * width,
            bytes_accessed=6 * 2**20,
            transcendentals=0,
        ),
        name="update",
    )(src, count, far, *blocks, acc, weight, z_old, dual, target, rho[None], beta[None])


def arrange(first, *refs):
    out = refs[-1]
    for d, part in enumerate(refs[:-1]):
        out[lax.rem(first() + d, len(refs) - 1)] = part[...]


def call_arrange(first, parts, name):
    shape = jax.ShapeDtypeStruct((len(parts), *parts[0].shape), parts[0].dtype)
    return pl.pallas_call(
        functools.partial(arrange, first),
        out_shape=shape,
        in_specs=[VMEM] * len(parts),
        out_specs=VMEM,
        compiler_params=pltpu.CompilerParams(vmem_limit_bytes=4 * 2**20),
        cost_estimate=SMALL,
        name=name,
    )(*parts)


def my_y():
    return lax.axis_index("wide") // 8


def my_z():
    return lax.rem(lax.axis_index("wide") // 2, 4)


def my_core():
    return lax.rem(lax.axis_index("wide"), 2)


def pair(mine, other, out):
    core = my_core()

    @pl.loop(0, mine.shape[0])
    def _(i):
        out[i, core] = mine[i]
        out[i, 1 - core] = other[i]


def call_pair(mine, other):
    groups, piece, hidden = mine.shape
    return pl.pallas_call(
        pair,
        out_shape=jax.ShapeDtypeStruct((groups, 2, piece, hidden), mine.dtype),
        in_specs=[VMEM, VMEM],
        out_specs=VMEM,
        compiler_params=pltpu.CompilerParams(vmem_limit_bytes=4 * 2**20),
        cost_estimate=SMALL,
        name="pair_rows",
    )(mine, other)


def whole_weight(parts, after):
    piece, hidden = parts.shape[1:]
    rows = [parts] + [along_y(parts, 4 - d) for d in (1, 2, 3)]
    after, *rows = lax.optimization_barrier((after, *rows))
    parts = call_arrange(my_y, rows, "rows_of_y").reshape(16, piece, hidden)
    return call_pair(parts, along_core(parts)).reshape(32 * piece, hidden), after


def reduced(keep, send, factor):
    y, z, _ = place(lax.axis_index("wide"))
    pick = functools.partial(lax.dynamic_index_in_dim, keepdims=False)
    f32 = lambda x: x.astype(jnp.float32)
    parts = (f32(keep) + f32(along_core(send))).astype(jnp.bfloat16)
    parts = parts.reshape(4, 4, *keep.shape[1:])
    halves = jnp.split(parts, 2, -1)

    def stage(halves, ways):
        sent = [
            [along(pick(half, (at + step) % 4, dim), step) for step in (1, 2, 3)]
            for half, (at, dim, along) in zip(halves, ways)
        ]
        return [
            sum(map(f32, arrived), f32(pick(half, at, dim))).astype(jnp.bfloat16)
            for half, arrived, (at, dim, _) in zip(halves, sent, ways)
        ]

    halves = stage(halves, [(z, 1, along_z), (y, 0, along_y)])
    halves = stage(halves, [(y, 0, along_y), (z, 0, along_z)])
    mine = jnp.concatenate(halves, -1)
    held = f32(mine)
    for step in (1, 2, 3):
        held = held + f32(along_comm(mine, step))
    return held * factor


def local(feats, tiles, tile_src, tile_count, request, z_old, dual, target, w_rows, rho, beta):
    comms, nodes, width = feats.shape
    piece, hidden = w_rows.shape
    asks = [along_comm(request, rel) for rel in (1, 2, 3)]
    first, w_rows, *asks = lax.optimization_barrier((feats[:, :, :EARLY], w_rows, *asks))
    early = along_comm(first, 2)
    beside = [along_z(w_rows, 4 - d) for d in (1, 2, 3)]
    chosen = call_choose(asks, feats)
    tiles, *both = lax.optimization_barrier((tiles, *beside, *chosen))
    beside, chosen = both[:3], both[3:]
    of_z = call_arrange(my_z, [w_rows, *beside], "rows_of_z")
    early, chosen[2] = lax.optimization_barrier((early, chosen[2]))
    heads = [along_comm(chosen[2 * n], 3 - n) for n in range(3)]
    near, far_off = [heads[0], heads[2]], [heads[1]]
    last1, last3, *near = lax.optimization_barrier((chosen[1], chosen[5], *near))
    last2, *far_off = lax.optimization_barrier((chosen[3], *far_off))
    heads = near[0], far_off[0], near[1]
    blocks = [along_comm(block, 3 - n) for n, block in enumerate((last1, last2, last3))]
    flat = lambda x: x.reshape(comms * nodes, hidden)
    acc, far, zs, ds, ts = call_own_products(
        tile_src, tile_count, request, feats, tiles, flat(z_old), flat(dual), flat(target)
    )
    weight, acc = whole_weight(of_z, acc)
    acc = call_head_products(tile_src, tile_count, request, far, early, heads, acc)
    new_z, new_dual, keep, send = call_update(
        tile_src, tile_count, far, blocks, acc, weight, zs, ds, ts, rho, beta, piece
    )
    total_nodes = comms * nodes * lax.axis_size("comm") * lax.axis_size("wide")
    grad = reduced(keep, send, 1.0 / math.sqrt(total_nodes))
    return new_z.reshape(z_old.shape), new_dual.reshape(z_old.shape), grad


def solution(mesh):
    split = P(("comm", "wide"))
    in_specs = (split,) * 8 + (P("wide"), P(), P())
    out_specs = (split, split, P("wide"))
    return jax.shard_map(local, mesh=mesh, in_specs=in_specs, out_specs=out_specs, check_vma=False)
```
